32 devices in a mesh: groups: 2 (over y), epoch: 4 (over z), strip: 2 (over x), band: 2 (over core).
Axes of the slice: x: 2, y: 2, z: 4, core: 2. Of those that a mesh axis runs over, the one named last changes fastest.
Arguments:
- template: bfloat16 [16, 48, 512], P(('groups', 'epoch'), 'strip', 'band'), parts along dimension 0, may hold values from -6 to 6
- science: float32 [32, 48, 512], P(('groups', 'epoch'), 'strip', 'band'), parts along dimension 0, may hold values from -6 to 6
- variance: float32 [32, 48, 512], P(('groups', 'epoch'), 'strip', 'band'), parts along dimension 0, may hold values from 2 to 40
- bad_mask: int32 [32, 48, 512], P(('groups', 'epoch'), 'strip', 'band'), parts along dimension 0, may hold values 0 or 1
- intersection: int32 [32], P('groups'), parts along dimension 0, may hold values from 0 to 7, as said below
- offsets: int32 [32, 2], P(('groups', 'epoch')), parts along dimension 0, may hold values from -4 to 4
- basis_index: int32 [32, 16], P(('groups', 'epoch')), parts along dimension 0, may hold values from 0 to 48
- coefficients: float32 [32, 16, 6], P(('groups', 'epoch')), parts along dimension 0, may hold values from -2 to 2
- basis: float32 [49, 19, 19], replicated, may hold values from -0.3125 to 0.3125
Outputs:
- residual_image: float32 [32, 48, 512], P(('groups', 'epoch'), 'strip', 'band'), parts along dimension 0
- coadd: float32 [16, 48, 512], P(('groups', 'epoch'), 'strip', 'band'), parts along dimension 0
The draws below stay inside these ranges and needn't reach their ends.
There are 2 independent parts, one for each index of `groups`. The reference program is written for one: setup_inputs(seed, part) draws one part's arguments, and reference() takes and returns one part's arrays. A program takes and returns all parts, laid end to end along the dimension named above; an argument that names none is the same for every part. Nothing has to cross between parts.
Inputs may be any that keep to these rules, and one draw needn't show every extreme that they name: `intersection`: exposure d * 4 + k (k < 4) covers a tile with index from (k) * 2 to (k) * 2 + 1, chosen at random among these.
All inputs are finite; a program needn't handle non-finite values. No bound on the sum of `bad_mask` on one device may be relied on, other than what follows from the above.
Results may differ from the reference program's by a relative error of at most 0.0018.
Values may be sent and summed in bfloat16 or wider, within the bound.
A program may use at most 64 MiB of HBM per device.

```python
import math
import jax
import jax.numpy as jnp
from jax import lax

KS = 19
HALF = 9
SHIFT = 4
NB = 49
NSEL = 16
NPOLY = 6
CAP = 1
TILE_DEV = 2
EXP_DEV = 4
EXPOSURES = 16
TILES = 8
HT = 48
WT = 512


def draw_intersection(key, part):
    position = jnp.arange(EXPOSURES, dtype=jnp.int32)
    owner = position % EXP_DEV // CAP
    choose = jax.random.randint(jax.random.fold_in(key, 17), (EXPOSURES,), 0, TILE_DEV)
    return (owner * TILE_DEV + choose).astype(jnp.int32)


def set_ends(drawn, rng, least, top_value):
    place = [jax.random.randint(jax.random.fold_in(rng, axis), (), 0, length) for axis, length in enumerate(drawn.shape)]
    widest = drawn.shape.index(max(drawn.shape))
    neighbour = place[:widest] + [(place[widest] + 1) % drawn.shape[widest]] + place[widest + 1:]
    return drawn.at[tuple(place)].set(least).at[tuple(neighbour)].set(top_value)


def block_scale(key, shape, shards, low, high):
    def one(dim, shards_of):
        heights = jax.random.uniform(jax.random.fold_in(jax.random.fold_in(key, 6), dim), (shards_of,), jnp.float32, low / len(shards), high / len(shards))
        return jnp.repeat(jnp.exp(heights), shape[dim] // shards_of).reshape((-1,) + (1,) * (len(shape) - dim - 1))

    loudness = one(*shards[0])
    for cut in shards[1:]:
        loudness = loudness * one(*cut)
    return loudness


def scatter_about(stream_key, shape, spread, reach, split=(), kind=jnp.bfloat16):
    drawn = jax.random.normal(stream_key, shape, jnp.float32) * spread
    if len(split) > 0:
        drawn = block_scale(stream_key, shape, split, -0.22, 0.18) * drawn
    return jnp.clip(drawn, min=-reach, max=reach).astype(kind)


def setup_inputs(seed: int = 0, part: int = 0) -> dict:
    streams_of = jax.random.split(jax.random.key(seed), 10)
    part_splits = jax.random.split(jax.random.fold_in(streams_of[9], part), 10)
    return {
        "template": scatter_about(part_splits[0], (TILES, HT, WT), 1.0, 6.0, ((0, 4), (1, 2), (2, 2))),
        "science": scatter_about(part_splits[1], (EXPOSURES, HT, WT), 1.0, 6.0, ((0, 4), (1, 2), (2, 2)), jnp.float32),
        "variance": jnp.clip(jnp.exp(math.log(40.0) - 2.9957323 * jax.random.uniform(part_splits[2], (EXPOSURES, HT, WT), jnp.float32) ** block_scale(part_splits[2], (EXPOSURES, HT, WT), ((0, 4), (1, 2), (2, 2)), -0.2, 0.2)), 2.0, 40.0),
        "bad_mask": set_ends((jax.random.randint(part_splits[3], (EXPOSURES, HT, WT), 0, 16) < 15).astype(jnp.int32), jax.random.fold_in(part_splits[3], 1), 0, 1),
        "intersection": draw_intersection(jax.random.fold_in(jax.random.fold_in(streams_of[9], part), 71), part),
        "offsets": set_ends(jax.random.randint(part_splits[5], (EXPOSURES, 2), 0 - SHIFT, SHIFT + 1), jax.random.fold_in(part_splits[5], 1), 0 - SHIFT, SHIFT).astype(jnp.int32),
        "basis_index": set_ends(jax.random.randint(part_splits[6], (EXPOSURES, NSEL), 0, NB), jax.random.fold_in(part_splits[6], 1), 0, NB - 1).astype(jnp.int32),
        "coefficients": scatter_about(part_splits[7], (EXPOSURES, NSEL, NPOLY), (0.5 / NSEL ** 0.5), 2.0, ((0, 4),), jnp.float32),
        "basis": scatter_about(streams_of[8], (NB, KS, KS), (KS * KS) ** -0.5, 0.3125, (), jnp.float32),
    }


highest = lax.Precision.HIGHEST


def poly_terms(rows_unit, cols_unit):
    ones = jnp.ones_like(rows_unit * cols_unit)
    return jnp.stack([ones, rows_unit * ones, cols_unit * ones, rows_unit * rows_unit * ones, rows_unit * cols_unit, cols_unit * cols_unit * ones])


def reference(template, science, variance, bad_mask, intersection, offsets, basis_index, coefficients, basis):
    height = template.shape[1]
    width = template.shape[2]
    rim = HALF + SHIFT
    padded = jnp.pad(template.astype(jnp.float32), ((0, 0), (rim, rim), (rim, rim)))
    picked = jnp.take(basis, basis_index, axis=0)
    kernels = jnp.einsum("ejp,ejab->epab", coefficients, picked, precision=highest).astype(jnp.bfloat16)
    kernels = lax.optimization_barrier(kernels).astype(jnp.float32)
    rows_unit = (2.0 * jnp.arange(height, dtype=jnp.float32) + 1.0) / height - 1.0
    cols_unit = (2.0 * jnp.arange(width, dtype=jnp.float32) + 1.0) / width - 1.0
    shapes = poly_terms(rows_unit[:, None], cols_unit[None, :])

    def one_model(item):
        tile, shift, kernel = item
        slab = lax.dynamic_index_in_dim(padded, tile.astype(jnp.int32), 0, keepdims=False)
        window = lax.dynamic_slice(slab, ((SHIFT + shift[0]).astype(jnp.int32), (SHIFT + shift[1]).astype(jnp.int32)), (height + 2 * HALF, width + 2 * HALF))
        conv = lax.conv_general_dilated(window[None, None], kernel[:, None], (1, 1), "VALID", precision=highest)[0]
        return jnp.sum(conv * shapes, axis=0)

    models = lax.map(one_model, (intersection, offsets, kernels))
    residual_image = science - models
    weight = bad_mask.astype(jnp.float32) / variance
    numer = jax.ops.segment_sum(weight * residual_image, intersection, num_segments=TILES)
    denom = jax.ops.segment_sum(weight, intersection, num_segments=TILES)
    return residual_image, numer / (denom + 1.0)
```

```python
import functools

import jax
import jax.numpy as jnp
from jax import lax
from jax.experimental import pallas as pl
from jax.experimental.pallas import tpu as pltpu
from jax.sharding import PartitionSpec as P

HALF = 9
SHIFT = 4
RIM = HALF + SHIFT
EDGE_ROWS = 16
LANES = 128
SLOT = 64

MESH = pl.DeviceIdType.MESH
STEPS = [(ds, db) for ds in (0, -1, 1) for db in (0, -1, 1)]


def kernel(
    sizes,
    intersection,
    offsets,
    basis_index,
    coefficients,
    template,
    science,
    variance,
    bad_mask,
    basis,
    residual,
    coadd,
    full,
    bottom,
    mid,
    top,
    low,
    kernel_rows,
    pairs,
    turns,
    toeplitz,
    weight,
    weight_out,
    weight_in,
    value_out,
    value_in,
    own_value,
    send_sem,
    recv_sem,
    back_send,
    back_recv,
):
    n_epoch, n_strip, n_band = sizes
    tile_dev, height, width = template.shape
    exp_dev = science.shape[0]
    n_sel, n_poly = coefficients.shape[1:]
    ks = basis.shape[1]
    group = lax.axis_index("groups")
    me = lax.axis_index("epoch")
    strip = lax.axis_index("strip")
    band = lax.axis_index("band")

    def target(epoch, ds, db):
        return (group, epoch, strip + ds, band + db)

    def there(ds, db):
        sides = []
        if ds < 0:
            sides.append(strip >= -ds)
        if ds > 0:
            sides.append(strip < n_strip - ds)
        if db < 0:
            sides.append(band >= -db)
        if db > 0:
            sides.append(band < n_band - db)
        return sides

    def guarded(sides, body):
        if not sides:
            body()
        elif len(sides) == 1:
            pl.when(sides[0])(body)
        else:
            pl.when(jnp.logical_and(sides[0], sides[1]))(body)

    barrier = pltpu.get_barrier_semaphore()
    for ds, db in STEPS:

        def greet(ds=ds, db=db):
            for step in range(n_epoch):
                if step == 0 and ds == 0 and db == 0:
                    continue
                epoch = lax.rem(me + step, n_epoch)
                pl.semaphore_signal(
                    barrier, inc=1, device_id=target(epoch, ds, db), device_id_type=MESH
                )

        guarded(there(ds, db), greet)

    for step in range(n_epoch):
        epoch = lax.rem(me + step, n_epoch)
        tile = intersection[epoch * exp_dev + me] - me * tile_dev
        chosen = template[jnp.clip(tile, 0, tile_dev - 1)]
        full[epoch] = chosen
        wide = chosen.astype(jnp.float32)
        bottom[epoch] = wide[height - EDGE_ROWS :].astype(jnp.bfloat16)
    mid[me, :, LANES : LANES + width] = full[me]

    zero = jnp.bfloat16(0)

    @pl.when(strip == 0)
    def _():
        top[...] = jnp.full(top.shape, zero)

    @pl.when(strip == n_strip - 1)
    def _():
        low[...] = jnp.full(low.shape, zero)

    for edge, lanes in ((band == 0, slice(0, LANES)), (band == n_band - 1, slice(LANES + width, None))):

        @pl.when(edge)
        def _(lanes=lanes):
            mid[:, :, lanes] = jnp.full(mid[:, :, lanes].shape, zero)

            @pl.when(strip > 0)
            def _():
                top[:, :, lanes] = jnp.full(top[:, :, lanes].shape, zero)

            @pl.when(strip < n_strip - 1)
            def _():
                low[:, :, lanes] = jnp.full(low[:, :, lanes].shape, zero)

    for exposure in range(exp_dev):
        value = bad_mask[exposure].astype(jnp.float32) / variance[exposure]
        weight[exposure] = value
        weight_out[exposure] = value.astype(jnp.bfloat16)

    kernel_rows[...] = jnp.zeros(kernel_rows.shape, jnp.float32)

    def sum_kernels(exposure, carry):
        sums = [jnp.zeros((ks, ks), jnp.float32) for _ in range(n_poly)]
        for j in range(n_sel):
            image = basis[basis_index[exposure, j]]
            for p in range(n_poly):
                sums[p] = sums[p] + coefficients[exposure, j, p] * image
        for p in range(n_poly):
            kernel_rows[exposure, p * LANES : p * LANES + ks, 0:ks] = sums[p]
        return carry

    lax.fori_loop(0, exp_dev, sum_kernels, 0)

    partners = n_epoch
    if n_strip > 1:
        near = jnp.minimum(strip, 1) + jnp.minimum(n_strip - 1 - strip, 1)
        partners = partners * (1 + near)
    if n_band > 1:
        near = jnp.minimum(band, 1) + jnp.minimum(n_band - 1 - band, 1)
        partners = partners * (1 + near)
    pl.semaphore_wait(barrier, partners - 1)

    def piece(step, ds, db, arriving):
        other = lax.rem(me + step, n_epoch)
        held = {0: slice(0, width), 1: slice(width - LANES, width), -1: slice(0, LANES)}[db]
        lands = {
            0: slice(LANES, LANES + width),
            1: slice(0, LANES),
            -1: slice(LANES + width, 2 * LANES + width),
        }[db]
        slot = other if arriving else me
        source = full.at[other, :, held]
        dest = mid
        if ds == 1:
            source, dest = bottom.at[other, :, held], top
        if ds == -1:
            source, dest = full.at[other, 0:EDGE_ROWS, held], low
        return pltpu.make_async_remote_copy(
            src_ref=source,
            dst_ref=dest.at[slot, :, lands],
            send_sem=send_sem.at[other, ds + 1, db + 1],
            recv_sem=recv_sem.at[slot, ds + 1, db + 1],
            device_id=target(other, ds, db),
            device_id_type=MESH,
        )

    for step in list(range(1, n_epoch)) + [0]:
        for ds, db in STEPS:
            if step == 0 and ds == 0 and db == 0:
                continue
            guarded(there(ds, db), lambda step=step, ds=ds, db=db: piece(step, ds, db, False).start())

    def back(which, out, into, step, arriving):
        other = lax.rem(me + step, n_epoch)
        slot = other if arriving else me
        return pltpu.make_async_remote_copy(
            src_ref=out.at[other],
            dst_ref=into.at[slot],
            send_sem=back_send.at[which, other],
            recv_sem=back_recv.at[which, slot],
            device_id=target(other, 0, 0),
            device_id_type=MESH,
        )

    for step in range(1, n_epoch):
        back(0, weight_out, weight_in, step, False).start()

    n_pairs = (ks + 1) // 2
    rows_all = pairs.shape[0]
    row = lax.broadcasted_iota(jnp.int32, (32, LANES), 0)
    col = lax.broadcasted_iota(jnp.int32, (32, LANES), 1)
    pick = jnp.where(row < 16, 2 * row, 2 * (row - 16) + 1)
    pick = (pick == col).astype(jnp.bfloat16)

    def build(exposure, carry):
        rows = kernel_rows[exposure].astype(jnp.bfloat16)
        turned = lax.dot_general(
            pick, rows, (((1,), (1,)), ((), ())), preferred_element_type=jnp.float32
        )
        for p in range(n_poly):
            block = turned[:, p * LANES : (p + 1) * LANES]
            both = block[:16] + pltpu.roll(block[16:], SLOT, 1)
            pairs[p * n_pairs : (p + 1) * n_pairs, :] = both[:n_pairs]
        shift = offsets[exposure, 0] + (SHIFT + EDGE_ROWS - RIM)
        every = pairs[...]
        for y in range(height):
            turns[y * rows_all : (y + 1) * rows_all, :] = pltpu.roll(every, shift + y, 1)
        for p in range(0, n_poly, 2):
            for q in range(n_pairs):
                halves = [
                    turns[pl.ds((p + h) * n_pairs + q, height, stride=rows_all), :]
                    for h in range(2)
                ]
                toeplitz[
                    exposure, p * height : (p + 2) * height, q * LANES : (q + 1) * LANES
                ] = jnp.concatenate(halves, axis=0).astype(jnp.bfloat16)
        return carry

    lax.fori_loop(0, exp_dev, build, 0)

    row = lax.broadcasted_iota(jnp.int32, (height, 1), 0) + strip * height
    col = lax.broadcasted_iota(jnp.int32, (1, width), 1) + band * width
    r = (2.0 * row.astype(jnp.float32) + 1.0) / (height * n_strip) - 1.0
    c = (2.0 * col.astype(jnp.float32) + 1.0) / (width * n_band) - 1.0
    r = jnp.broadcast_to(r, (height, width))
    c = jnp.broadcast_to(c, (height, width))

    def arrive(step):
        for ds, db in STEPS:
            if ds == 0 and db == 0 and step == 0:
                continue
            guarded(
                there(-ds, -db),
                lambda ds=ds, db=db: piece(step, ds, db, True).wait_recv(),
            )

    for step in range(n_epoch):
        k = lax.rem(me + step, n_epoch)
        arrive(step)
        slab = jnp.concatenate(
            [
                top[k].astype(jnp.float32),
                mid[k].astype(jnp.float32),
                low[k].astype(jnp.float32),
                jnp.zeros((SLOT - height - 2 * EDGE_ROWS, width + 2 * LANES), jnp.float32),
            ],
            axis=0,
        )
        total = width + 2 * LANES
        slab = pltpu.roll(slab, total - (LANES - RIM + SHIFT) - offsets[k, 1], 1)
        slab = slab[:, : width + LANES].astype(jnp.bfloat16)
        conv = jnp.zeros((n_poly * height, width), jnp.float32)
        for first in range(0, ks, 4):
            columns = range(first, min(first + 4, ks))
            stacked = jnp.concatenate([slab[:, b : b + width] for b in columns], axis=0)
            conv = conv + jnp.dot(
                toeplitz[k, :, first * SLOT : (first + len(columns)) * SLOT],
                stacked,
                preferred_element_type=jnp.float32,
            )
        q = [conv[p * height : (p + 1) * height] for p in range(n_poly)]
        model = q[0] + r * (q[1] + r * q[3] + c * q[4]) + c * (q[2] + c * q[5])
        left = science[k] - model
        residual[k] = left
        value = weight[k] * left
        if step == 0:
            own_value[...] = value
        else:
            value_out[k] = value.astype(jnp.bfloat16)
            back(1, value_out, value_in, step, False).start()

    numer = [None] * tile_dev
    denom = [None] * tile_dev
    for step in range(n_epoch):
        k = lax.rem(me + step, n_epoch)
        tile = intersection[k * exp_dev + me] - me * tile_dev
        if step == 0:
            upper, under = own_value[...], weight[me]
        else:
            back(0, weight_out, weight_in, step, True).wait_recv()
            back(1, value_out, value_in, step, True).wait_recv()
            upper = value_in[k].astype(jnp.float32)
            under = weight_in[k].astype(jnp.float32)
        for t in range(tile_dev):
            here = (tile == t).astype(jnp.float32)
            numer[t] = upper * here if step == 0 else numer[t] + upper * here
            denom[t] = under * here if step == 0 else denom[t] + under * here
    for t in range(tile_dev):
        coadd[t] = numer[t] / (denom[t] + 1.0)

    for step in range(n_epoch):
        for ds, db in STEPS:
            if step == 0 and ds == 0 and db == 0:
                continue
            guarded(
                there(ds, db),
                lambda step=step, ds=ds, db=db: piece(step, ds, db, False).wait_send(),
            )
        if step > 0:
            back(0, weight_out, weight_in, step, False).wait_send()
            back(1, value_out, value_in, step, False).wait_send()


def local(sizes, template, science, variance, bad_mask, intersection, offsets, basis_index, coefficients, basis):
    n_epoch = sizes[0]
    tile_dev, height, width = template.shape
    exp_dev = science.shape[0]
    assert exp_dev == n_epoch
    n_poly = coefficients.shape[2]
    ks = basis.shape[1]
    lanes_all = width + 2 * LANES
    n_pairs = (ks + 1) // 2
    rows_all = -(-n_poly * n_pairs // 8) * 8
    smem = pl.BlockSpec(memory_space=pltpu.SMEM)
    vmem = pl.BlockSpec(memory_space=pltpu.VMEM)
    bf16, f32 = jnp.bfloat16, jnp.float32
    dma = pltpu.SemaphoreType.DMA
    return pl.pallas_call(
        functools.partial(kernel, sizes),
        out_shape=(
            jax.ShapeDtypeStruct(science.shape, f32),
            jax.ShapeDtypeStruct(template.shape, f32),
        ),
        in_specs=[smem] * 4 + [vmem] * 5,
        out_specs=(vmem, vmem),
        scratch_shapes=[
            pltpu.VMEM((n_epoch, height, width), bf16),
            pltpu.VMEM((n_epoch, EDGE_ROWS, width), bf16),
            pltpu.VMEM((exp_dev, height, lanes_all), bf16),
            pltpu.VMEM((exp_dev, EDGE_ROWS, lanes_all), bf16),
            pltpu.VMEM((exp_dev, EDGE_ROWS, lanes_all), bf16),
            pltpu.VMEM((exp_dev, n_poly * LANES, LANES), f32),
            pltpu.VMEM((rows_all, LANES), f32),
            pltpu.VMEM((height * rows_all, LANES), f32),
            pltpu.VMEM((exp_dev, n_poly * height, n_pairs * LANES), bf16),
            pltpu.VMEM((exp_dev, height, width), f32),
            pltpu.VMEM((exp_dev, height, width), bf16),
            pltpu.VMEM((exp_dev, height, width), bf16),
            pltpu.VMEM((exp_dev, height, width), bf16),
            pltpu.VMEM((exp_dev, height, width), bf16),
            pltpu.VMEM((height, width), f32),
            dma((n_epoch, 3, 3)),
            dma((n_epoch, 3, 3)),
            dma((2, n_epoch)),
            dma((2, n_epoch)),
        ],
        compiler_params=pltpu.CompilerParams(collective_id=0, has_side_effects=True),
    )(
        intersection, offsets, basis_index, coefficients,
        template, science, variance, bad_mask, basis,
    )


def solution(mesh):
    sizes = (mesh.shape["epoch"], mesh.shape["strip"], mesh.shape["band"])
    image = P(("groups", "epoch"), "strip", "band")
    split = ("groups", "epoch")
    in_specs = (
        image, image, image, image, P("groups"),
        P(split, None), P(split, None), P(split, None, None), P(),
    )
    return jax.shard_map(
        functools.partial(local, sizes),
        mesh=mesh,
        in_specs=in_specs,
        out_specs=(image, image),
        check_vma=False,
    )
```

```python
import functools

import jax
import jax.numpy as jnp
from jax import lax
from jax.experimental import pallas as pl
from jax.experimental.pallas import tpu as pltpu
from jax.sharding import PartitionSpec as P

HALF = 9
SHIFT = 4
RIM = HALF + SHIFT
EDGE_ROWS = 16
LANES = 128
SLOT = 64

MESH = pl.DeviceIdType.MESH
STEPS = [(ds, db) for ds in (0, -1, 1) for db in (0, -1, 1)]


def kernel(
    sizes,
    intersection,
    offsets,
    basis_index,
    coefficients,
    template,
    science_hbm,
    variance_hbm,
    bad_mask_hbm,
    basis_hbm,
    residual_out,
    coadd_out,
    science,
    variance,
    bad_mask,
    basis,
    residual,
    coadd,
    full,
    bottom,
    mid,
    top,
    low,
    turned_basis,
    pairs,
    turns,
    toeplitz,
    weight,
    weight_in,
    value_out,
    value_in,
    own_value,
    local_sem,
    send_sem,
    recv_sem,
    back_send,
    back_recv,
):
    n_epoch, n_strip, n_band = sizes
    tile_dev, height, width = template.shape
    exp_dev = science.shape[0]
    n_poly, _, n_sel = coefficients.shape
    ks, _, n_basis = basis.shape
    group = lax.axis_index("groups")
    me = lax.axis_index("epoch")
    strip = lax.axis_index("strip")
    band = lax.axis_index("band")

    def target(epoch, ds, db):
        return (group, epoch, strip + ds, band + db)

    def there(ds, db):
        sides = []
        if ds < 0:
            sides.append(strip >= -ds)
        if ds > 0:
            sides.append(strip < n_strip - ds)
        if db < 0:
            sides.append(band >= -db)
        if db > 0:
            sides.append(band < n_band - db)
        return sides

    def guarded(sides, body):
        if not sides:
            body()
        elif len(sides) == 1:
            pl.when(sides[0])(body)
        else:
            pl.when(jnp.logical_and(sides[0], sides[1]))(body)

    barrier = pltpu.get_barrier_semaphore()
    for ds, db in STEPS:

        def greet(ds=ds, db=db):
            for step in range(n_epoch):
                if step == 0 and ds == 0 and db == 0:
                    continue
                epoch = lax.rem(me + step, n_epoch)
                pl.semaphore_signal(
                    barrier, inc=1, device_id=target(epoch, ds, db), device_id_type=MESH
                )

        guarded(there(ds, db), greet)

    loads = [
        pltpu.make_async_copy(held, here, local_sem.at[i])
        for i, (held, here) in enumerate(
            (
                (basis_hbm, basis),
                (variance_hbm, variance),
                (bad_mask_hbm, bad_mask),
                (science_hbm, science),
            )
        )
    ]
    for load in loads:
        load.start()

    for step in range(n_epoch):
        epoch = lax.rem(me + step, n_epoch)
        tile = intersection[epoch * exp_dev + me] - me * tile_dev
        chosen = template[jnp.clip(tile, 0, tile_dev - 1)]
        full[epoch] = chosen
        wide = chosen.astype(jnp.float32)
        bottom[epoch] = wide[height - EDGE_ROWS :].astype(jnp.bfloat16)
    mid[me, :, LANES : LANES + width] = full[me]

    zero = jnp.bfloat16(0)

    @pl.when(strip == 0)
    def _():
        top[...] = jnp.full(top.shape, zero)

    @pl.when(strip == n_strip - 1)
    def _():
        low[...] = jnp.full(low.shape, zero)

    for edge, lanes in ((band == 0, slice(0, LANES)), (band == n_band - 1, slice(LANES + width, None))):

        @pl.when(edge)
        def _(lanes=lanes):
            mid[:, :, lanes] = jnp.full(mid[:, :, lanes].shape, zero)

            @pl.when(strip > 0)
            def _():
                top[:, :, lanes] = jnp.full(top[:, :, lanes].shape, zero)

            @pl.when(strip < n_strip - 1)
            def _():
                low[:, :, lanes] = jnp.full(low[:, :, lanes].shape, zero)

    lane = lax.broadcasted_iota(jnp.int32, (n_poly, LANES), 1)
    mixes = []
    for exposure in range(exp_dev):
        coefs = coefficients[:, exposure, :]
        mix = jnp.zeros((n_poly, LANES), jnp.float32)
        for j in range(n_sel):
            mix = mix + jnp.where(lane == basis_index[exposure, j], coefs[:, j : j + 1], 0.0)
        mixes.append(mix)
        if n_poly < 8:
            mixes.append(jnp.zeros((8 - n_poly, LANES), jnp.float32))
    mixes = jnp.concatenate(mixes, axis=0)

    n_pairs = (ks + 1) // 2
    rows_all = pairs.shape[0] // exp_dev
    turned_basis[...] = jnp.zeros(turned_basis.shape, jnp.float32)
    loads[0].wait()
    for b in range(ks):
        turned_basis[b * SLOT : b * SLOT + ks, 0:n_basis] = basis[:, b, :]

    for q in range(0, n_pairs, 2):
        some = lax.dot_general(
            mixes,
            turned_basis[q * LANES : (q + 2) * LANES, :],
            (((1,), (1,)), ((), ())),
            precision=lax.Precision.HIGHEST,
            preferred_element_type=jnp.float32,
        )
        some = some.astype(jnp.bfloat16).astype(jnp.float32)
        for half in range(2):
            for exposure in range(exp_dev):
                at = exposure * rows_all + (q + half) * n_poly
                pairs[at : at + n_poly, :] = some[
                    exposure * 8 : exposure * 8 + n_poly, half * LANES : (half + 1) * LANES
                ]

    loads[1].wait()
    loads[2].wait()
    for exposure in range(exp_dev):
        weight[exposure] = bad_mask[exposure].astype(jnp.float32) / variance[exposure]

    partners = n_epoch
    if n_strip > 1:
        near = jnp.minimum(strip, 1) + jnp.minimum(n_strip - 1 - strip, 1)
        partners = partners * (1 + near)
    if n_band > 1:
        near = jnp.minimum(band, 1) + jnp.minimum(n_band - 1 - band, 1)
        partners = partners * (1 + near)
    pl.semaphore_wait(barrier, partners - 1)

    def piece(step, ds, db, arriving):
        other = lax.rem(me + step, n_epoch)
        held = {0: slice(0, width), 1: slice(width - LANES, width), -1: slice(0, LANES)}[db]
        lands = {
            0: slice(LANES, LANES + width),
            1: slice(0, LANES),
            -1: slice(LANES + width, 2 * LANES + width),
        }[db]
        slot = other if arriving else me
        source = full.at[other, :, held]
        dest = mid
        if ds == 1:
            source, dest = bottom.at[other, :, held], top
        if ds == -1:
            source, dest = full.at[other, 0:EDGE_ROWS, held], low
        return pltpu.make_async_remote_copy(
            src_ref=source,
            dst_ref=dest.at[slot, :, lands],
            send_sem=send_sem.at[other, ds + 1, db + 1],
            recv_sem=recv_sem.at[slot, ds + 1, db + 1],
            device_id=target(other, ds, db),
            device_id_type=MESH,
        )

    for step in list(range(1, n_epoch)) + [0]:
        for ds, db in STEPS:
            if step == 0 and ds == 0 and db == 0:
                continue
            guarded(there(ds, db), lambda step=step, ds=ds, db=db: piece(step, ds, db, False).start())

    def back(which, out, into, step, arriving):
        other = lax.rem(me + step, n_epoch)
        slot = other if arriving else me
        return pltpu.make_async_remote_copy(
            src_ref=out.at[other],
            dst_ref=into.at[slot],
            send_sem=back_send.at[which, other],
            recv_sem=back_recv.at[which, slot],
            device_id=target(other, 0, 0),
            device_id_type=MESH,
        )

    for step in range(1, n_epoch):
        back(0, weight, weight_in, step, False).start()

    def build(exposure, carry):
        shift = offsets[0, exposure] + (SHIFT + EDGE_ROWS - RIM)
        every = pairs[pl.ds(pl.multiple_of(exposure * rows_all, 8), rows_all), :]
        for y in range(height):
            turns[y * rows_all : (y + 1) * rows_all, :] = pltpu.roll(every, shift + y, 1)
        for p in range(0, n_poly, 2):
            for q in range(n_pairs):
                halves = [
                    turns[pl.ds(q * n_poly + p + h, height, stride=rows_all), :]
                    for h in range(2)
                ]
                toeplitz[
                    exposure, p * height : (p + 2) * height, q * LANES : (q + 1) * LANES
                ] = jnp.concatenate(halves, axis=0).astype(jnp.bfloat16)
        return carry

    lax.fori_loop(0, exp_dev, build, 0)

    row = lax.broadcasted_iota(jnp.int32, (height, 1), 0) + strip * height
    col = lax.broadcasted_iota(jnp.int32, (1, width), 1) + band * width
    r = (2.0 * row.astype(jnp.float32) + 1.0) / (height * n_strip) - 1.0
    c = (2.0 * col.astype(jnp.float32) + 1.0) / (width * n_band) - 1.0
    r = jnp.broadcast_to(r, (height, width))
    c = jnp.broadcast_to(c, (height, width))

    def arrive(step):
        for ds, db in STEPS:
            if ds == 0 and db == 0 and step == 0:
                continue
            guarded(
                there(-ds, -db),
                lambda ds=ds, db=db: piece(step, ds, db, True).wait_recv(),
            )

    loads[3].wait()
    for step in range(n_epoch):
        k = lax.rem(me + step, n_epoch)
        arrive(step)
        slab = jnp.concatenate(
            [
                top[k].astype(jnp.float32),
                mid[k].astype(jnp.float32),
                low[k].astype(jnp.float32),
                jnp.zeros((SLOT - height - 2 * EDGE_ROWS, width + 2 * LANES), jnp.float32),
            ],
            axis=0,
        )
        total = width + 2 * LANES
        slab = pltpu.roll(slab, total - (LANES - RIM + SHIFT) - offsets[1, k], 1)
        slab = slab[:, : width + LANES].astype(jnp.bfloat16)
        conv = jnp.zeros((n_poly * height, width), jnp.float32)
        for first in range(0, ks, 4):
            columns = range(first, min(first + 4, ks))
            stacked = jnp.concatenate([slab[:, b : b + width] for b in columns], axis=0)
            conv = conv + jnp.dot(
                toeplitz[k, :, first * SLOT : (first + len(columns)) * SLOT],
                stacked,
                preferred_element_type=jnp.float32,
            )
        q = [conv[p * height : (p + 1) * height] for p in range(n_poly)]
        model = q[0] + r * (q[1] + r * q[3] + c * q[4]) + c * (q[2] + c * q[5])
        left = science[k] - model
        residual[k] = left
        pltpu.make_async_copy(residual.at[k], residual_out.at[k], local_sem.at[4 + k]).start()
        value = weight[k] * left
        if step == 0:
            own_value[...] = value
        else:
            value_out[k] = value
            back(1, value_out, value_in, step, False).start()

    numer = [None] * tile_dev
    denom = [None] * tile_dev
    for step in range(n_epoch):
        k = lax.rem(me + step, n_epoch)
        tile = intersection[k * exp_dev + me] - me * tile_dev
        if step == 0:
            upper, under = own_value[...], weight[me]
        else:
            back(0, weight, weight_in, step, True).wait_recv()
            back(1, value_out, value_in, step, True).wait_recv()
            upper = value_in[k]
            under = weight_in[k]
        for t in range(tile_dev):
            here = (tile == t).astype(jnp.float32)
            numer[t] = upper * here if step == 0 else numer[t] + upper * here
            denom[t] = under * here if step == 0 else denom[t] + under * here
    for t in range(tile_dev):
        coadd[t] = numer[t] / (denom[t] + 1.0)
    last = pltpu.make_async_copy(coadd, coadd_out, local_sem.at[4 + n_epoch])
    last.start()

    for step in range(n_epoch):
        for ds, db in STEPS:
            if step == 0 and ds == 0 and db == 0:
                continue
            guarded(
                there(ds, db),
                lambda step=step, ds=ds, db=db: piece(step, ds, db, False).wait_send(),
            )
        if step > 0:
            back(0, weight, weight_in, step, False).wait_send()
            back(1, value_out, value_in, step, False).wait_send()
        k = lax.rem(me + step, n_epoch)
        pltpu.make_async_copy(residual.at[k], residual_out.at[k], local_sem.at[4 + k]).wait()
    last.wait()


def local(sizes, template, science, variance, bad_mask, intersection, offsets, basis_index, coefficients, basis):
    n_epoch = sizes[0]
    tile_dev, height, width = template.shape
    exp_dev = science.shape[0]
    assert exp_dev == n_epoch
    n_poly = coefficients.shape[2]
    ks = basis.shape[1]
    lanes_all = width + 2 * LANES
    n_pairs = (ks + 1) // 2
    rows_all = -(-n_poly * n_pairs // 8) * 8
    smem = pl.BlockSpec(memory_space=pltpu.SMEM)
    vmem = pl.BlockSpec(memory_space=pltpu.VMEM)
    free = pl.BlockSpec(memory_space=pl.ANY)
    bf16, f32 = jnp.bfloat16, jnp.float32
    dma = pltpu.SemaphoreType.DMA
    offsets = offsets.T
    coefficients = coefficients.transpose(2, 0, 1)
    basis = basis.transpose(1, 2, 0)
    return pl.pallas_call(
        functools.partial(kernel, sizes),
        out_shape=(
            jax.ShapeDtypeStruct(science.shape, f32),
            jax.ShapeDtypeStruct(template.shape, f32),
        ),
        in_specs=[smem] * 3 + [vmem] * 2 + [free] * 4,
        out_specs=(free, free),
        scratch_shapes=[
            pltpu.VMEM(science.shape, f32),
            pltpu.VMEM(science.shape, f32),
            pltpu.VMEM(science.shape, jnp.int32),
            pltpu.VMEM(basis.shape, f32),
            pltpu.VMEM(science.shape, f32),
            pltpu.VMEM(template.shape, f32),
            pltpu.VMEM((n_epoch, height, width), bf16),
            pltpu.VMEM((n_epoch, EDGE_ROWS, width), bf16),
            pltpu.VMEM((exp_dev, height, lanes_all), bf16),
            pltpu.VMEM((exp_dev, EDGE_ROWS, lanes_all), bf16),
            pltpu.VMEM((exp_dev, EDGE_ROWS, lanes_all), bf16),
            pltpu.VMEM((n_pairs * LANES, LANES), f32),
            pltpu.VMEM((exp_dev * rows_all, LANES), f32),
            pltpu.VMEM((height * rows_all, LANES), f32),
            pltpu.VMEM((exp_dev, n_poly * height, n_pairs * LANES), bf16),
            pltpu.VMEM((exp_dev, height, width), f32),
            pltpu.VMEM((exp_dev, height, width), f32),
            pltpu.VMEM((exp_dev, height, width), f32),
            pltpu.VMEM((exp_dev, height, width), f32),
            pltpu.VMEM((height, width), f32),
            dma((5 + n_epoch,)),
            dma((n_epoch, 3, 3)),
            dma((n_epoch, 3, 3)),
            dma((2, n_epoch)),
            dma((2, n_epoch)),
        ],
        compiler_params=pltpu.CompilerParams(collective_id=0, has_side_effects=True),
    )(
        intersection, offsets, basis_index, coefficients,
        template, science, variance, bad_mask, basis,
    )


def solution(mesh):
    sizes = (mesh.shape["epoch"], mesh.shape["strip"], mesh.shape["band"])
    image = P(("groups", "epoch"), "strip", "band")
    split = ("groups", "epoch")
    in_specs = (
        image, image, image, image, P("groups"),
        P(split, None), P(split, None), P(split, None, None), P(),
    )
    return jax.shard_map(
        functools.partial(local, sizes),
        mesh=mesh,
        in_specs=in_specs,
        out_specs=(image, image),
        check_vma=False,
    )
```

```python
import functools

import jax
import jax.numpy as jnp
from jax import lax
from jax.experimental import pallas as pl
from jax.experimental.pallas import tpu as pltpu
from jax.sharding import PartitionSpec as P

HALF = 9
SHIFT = 4
RIM = HALF + SHIFT
EDGE_ROWS = 16
LANES = 128
SLOT = 64

MESH = pl.DeviceIdType.MESH
STEPS = [(ds, db) for ds in (0, -1, 1) for db in (0, -1, 1)]


def kernel(
    sizes,
    intersection_hbm,
    offsets_hbm,
    basis_index_hbm,
    coefficients_hbm,
    template_hbm,
    science_hbm,
    variance_hbm,
    bad_mask_hbm,
    basis_hbm,
    residual_out,
    coadd_out,
    intersection,
    offsets,
    basis_index,
    coefficients,
    template,
    science,
    variance,
    bad_mask,
    basis,
    residual,
    coadd,
    full,
    bottom,
    mid,
    top,
    low,
    turned_basis,
    pairs,
    turns,
    toeplitz,
    weight,
    weight_in,
    value_out,
    value_in,
    own_value,
    local_sem,
    send_sem,
    recv_sem,
    back_send,
    back_recv,
):
    n_epoch, n_strip, n_band = sizes
    tile_dev, height, width = template.shape
    exp_dev = science.shape[0]
    n_poly, _, n_sel = coefficients.shape
    ks, _, n_basis = basis.shape
    group = lax.axis_index("groups")
    me = lax.axis_index("epoch")
    strip = lax.axis_index("strip")
    band = lax.axis_index("band")

    side = 2 * lax.div(2 * me, n_epoch) - 1

    def away(step):
        return lax.rem(me + n_epoch + side * step, n_epoch)

    def target(epoch, ds, db):
        return (group, epoch, strip + ds, band + db)

    def there(ds, db):
        sides = []
        if ds < 0:
            sides.append(strip >= -ds)
        if ds > 0:
            sides.append(strip < n_strip - ds)
        if db < 0:
            sides.append(band >= -db)
        if db > 0:
            sides.append(band < n_band - db)
        return sides

    def guarded(sides, body):
        if not sides:
            body()
        elif len(sides) == 1:
            pl.when(sides[0])(body)
        else:
            pl.when(jnp.logical_and(sides[0], sides[1]))(body)

    loads = [
        pltpu.make_async_copy(held, here, local_sem.at[i])
        for i, (held, here) in enumerate(
            (
                (basis_hbm, basis),
                (variance_hbm, variance),
                (bad_mask_hbm, bad_mask),
                (science_hbm, science),
                (intersection_hbm, intersection),
                (template_hbm, template),
                (basis_index_hbm, basis_index),
                (coefficients_hbm, coefficients),
                (offsets_hbm, offsets),
            )
        )
    ]
    for i in (4, 5, 6, 7, 0, 1, 2, 3, 8):
        loads[i].start()

    barrier = pltpu.get_barrier_semaphore()
    for ds, db in STEPS:

        def greet(ds=ds, db=db):
            for step in range(n_epoch):
                if step == 0 and ds == 0 and db == 0:
                    continue
                epoch = away(step)
                pl.semaphore_signal(
                    barrier, inc=1, device_id=target(epoch, ds, db), device_id_type=MESH
                )

        guarded(there(ds, db), greet)

    loads[4].wait()
    loads[5].wait()
    for step in range(n_epoch):
        epoch = away(step)
        tile = intersection[epoch * exp_dev + me] - me * tile_dev
        chosen = template[jnp.clip(tile, 0, tile_dev - 1)]
        full[epoch] = chosen
        wide = chosen.astype(jnp.float32)
        bottom[epoch] = wide[height - EDGE_ROWS :].astype(jnp.bfloat16)
    mid[me, :, LANES : LANES + width] = full[me]

    zero = jnp.bfloat16(0)

    @pl.when(strip == 0)
    def _():
        top[...] = jnp.full(top.shape, zero)

    @pl.when(strip == n_strip - 1)
    def _():
        low[...] = jnp.full(low.shape, zero)

    for edge, lanes in ((band == 0, slice(0, LANES)), (band == n_band - 1, slice(LANES + width, None))):

        @pl.when(edge)
        def _(lanes=lanes):
            mid[:, :, lanes] = jnp.full(mid[:, :, lanes].shape, zero)

            @pl.when(strip > 0)
            def _():
                top[:, :, lanes] = jnp.full(top[:, :, lanes].shape, zero)

            @pl.when(strip < n_strip - 1)
            def _():
                low[:, :, lanes] = jnp.full(low[:, :, lanes].shape, zero)

    loads[6].wait()
    loads[7].wait()
    lane = lax.broadcasted_iota(jnp.int32, (n_poly, LANES), 1)
    mixes = []
    for exposure in range(exp_dev):
        coefs = coefficients[:, exposure, :]
        mix = jnp.zeros((n_poly, LANES), jnp.float32)
        for j in range(n_sel):
            mix = mix + jnp.where(lane == basis_index[exposure, j], coefs[:, j : j + 1], 0.0)
        mixes.append(mix)
        if n_poly < 8:
            mixes.append(jnp.zeros((8 - n_poly, LANES), jnp.float32))
    mixes = jnp.concatenate(mixes, axis=0)

    n_pairs = (ks + 1) // 2
    rows_all = pairs.shape[0] // exp_dev
    turned_basis[...] = jnp.zeros(turned_basis.shape, jnp.float32)
    loads[0].wait()
    for b in range(ks):
        turned_basis[b * SLOT : b * SLOT + ks, 0:n_basis] = basis[:, b, :]

    for q in range(0, n_pairs, 2):
        some = lax.dot_general(
            mixes,
            turned_basis[q * LANES : (q + 2) * LANES, :],
            (((1,), (1,)), ((), ())),
            precision=lax.Precision.HIGHEST,
            preferred_element_type=jnp.float32,
        )
        some = some.astype(jnp.bfloat16).astype(jnp.float32)
        for half in range(2):
            for exposure in range(exp_dev):
                at = exposure * rows_all + (q + half) * n_poly
                pairs[at : at + n_poly, :] = some[
                    exposure * 8 : exposure * 8 + n_poly, half * LANES : (half + 1) * LANES
                ]

    loads[1].wait()
    loads[2].wait()
    for exposure in range(exp_dev):
        weight[exposure] = bad_mask[exposure].astype(jnp.float32) / variance[exposure]

    partners = n_epoch
    if n_strip > 1:
        near = jnp.minimum(strip, 1) + jnp.minimum(n_strip - 1 - strip, 1)
        partners = partners * (1 + near)
    if n_band > 1:
        near = jnp.minimum(band, 1) + jnp.minimum(n_band - 1 - band, 1)
        partners = partners * (1 + near)
    pl.semaphore_wait(barrier, partners - 1)

    def piece(step, ds, db, arriving):
        other = away(step)
        held = {0: slice(0, width), 1: slice(width - LANES, width), -1: slice(0, LANES)}[db]
        lands = {
            0: slice(LANES, LANES + width),
            1: slice(0, LANES),
            -1: slice(LANES + width, 2 * LANES + width),
        }[db]
        slot = other if arriving else me
        source = full.at[other, :, held]
        dest = mid
        if ds == 1:
            source, dest = bottom.at[other, :, held], top
        if ds == -1:
            source, dest = full.at[other, 0:EDGE_ROWS, held], low
        return pltpu.make_async_remote_copy(
            src_ref=source,
            dst_ref=dest.at[slot, :, lands],
            send_sem=send_sem.at[other, ds + 1, db + 1],
            recv_sem=recv_sem.at[slot, ds + 1, db + 1],
            device_id=target(other, ds, db),
            device_id_type=MESH,
        )

    for step in list(range(1, n_epoch)) + [0]:
        for ds, db in STEPS:
            if step == 0 and ds == 0 and db == 0:
                continue
            guarded(there(ds, db), lambda step=step, ds=ds, db=db: piece(step, ds, db, False).start())

    def back(which, out, into, step, arriving):
        other = away(step)
        slot = other if arriving else me
        return pltpu.make_async_remote_copy(
            src_ref=out.at[other],
            dst_ref=into.at[slot],
            send_sem=back_send.at[which, other],
            recv_sem=back_recv.at[which, slot],
            device_id=target(other, 0, 0),
            device_id_type=MESH,
        )

    for step in range(1, n_epoch):
        back(0, weight, weight_in, step, False).start()

    loads[8].wait()

    def build(exposure, carry):
        shift = offsets[0, exposure] + (SHIFT + EDGE_ROWS - RIM)
        every = pairs[pl.ds(pl.multiple_of(exposure * rows_all, 8), rows_all), :]
        for y in range(height):
            turns[y * rows_all : (y + 1) * rows_all, :] = pltpu.roll(every, shift + y, 1)
        for p in range(0, n_poly, 2):
            for q in range(n_pairs):
                halves = [
                    turns[pl.ds(q * n_poly + p + h, height, stride=rows_all), :]
                    for h in range(2)
                ]
                toeplitz[
                    exposure, p * height : (p + 2) * height, q * LANES : (q + 1) * LANES
                ] = jnp.concatenate(halves, axis=0).astype(jnp.bfloat16)
        return carry

    lax.fori_loop(0, exp_dev, build, 0)

    row = lax.broadcasted_iota(jnp.int32, (height, 1), 0) + strip * height
    col = lax.broadcasted_iota(jnp.int32, (1, width), 1) + band * width
    r = (2.0 * row.astype(jnp.float32) + 1.0) / (height * n_strip) - 1.0
    c = (2.0 * col.astype(jnp.float32) + 1.0) / (width * n_band) - 1.0
    r = jnp.broadcast_to(r, (height, width))
    c = jnp.broadcast_to(c, (height, width))

    def arrive(step):
        for ds, db in STEPS:
            if ds == 0 and db == 0 and step == 0:
                continue
            guarded(
                there(-ds, -db),
                lambda ds=ds, db=db: piece(step, ds, db, True).wait_recv(),
            )

    loads[3].wait()
    for step in range(n_epoch):
        k = away(step)
        arrive(step)
        slab = jnp.concatenate(
            [
                top[k].astype(jnp.float32),
                mid[k].astype(jnp.float32),
                low[k].astype(jnp.float32),
                jnp.zeros((SLOT - height - 2 * EDGE_ROWS, width + 2 * LANES), jnp.float32),
            ],
            axis=0,
        )
        total = width + 2 * LANES
        slab = pltpu.roll(slab, total - (LANES - RIM + SHIFT) - offsets[1, k], 1)
        slab = slab[:, : width + LANES].astype(jnp.bfloat16)
        conv = jnp.zeros((n_poly * height, width), jnp.float32)
        for first in range(0, ks, 4):
            columns = range(first, min(first + 4, ks))
            stacked = jnp.concatenate([slab[:, b : b + width] for b in columns], axis=0)
            conv = conv + jnp.dot(
                toeplitz[k, :, first * SLOT : (first + len(columns)) * SLOT],
                stacked,
                preferred_element_type=jnp.float32,
            )
        q = [conv[p * height : (p + 1) * height] for p in range(n_poly)]
        model = q[0] + r * (q[1] + r * q[3] + c * q[4]) + c * (q[2] + c * q[5])
        left = science[k] - model
        residual[k] = left
        pltpu.make_async_copy(residual.at[k], residual_out.at[k], local_sem.at[9 + k]).start()
        value = weight[k] * left
        if step == 0:
            own_value[...] = value
        else:
            value_out[k] = value
            back(1, value_out, value_in, step, False).start()

    numer = [None] * tile_dev
    denom = [None] * tile_dev
    for step in range(n_epoch):
        k = away(step)
        tile = intersection[k * exp_dev + me] - me * tile_dev
        if step == 0:
            upper, under = own_value[...], weight[me]
        else:
            back(0, weight, weight_in, step, True).wait_recv()
            back(1, value_out, value_in, step, True).wait_recv()
            upper = value_in[k]
            under = weight_in[k]
        for t in range(tile_dev):
            here = (tile == t).astype(jnp.float32)
            numer[t] = upper * here if step == 0 else numer[t] + upper * here
            denom[t] = under * here if step == 0 else denom[t] + under * here
    for t in range(tile_dev):
        coadd[t] = numer[t] / (denom[t] + 1.0)
    last = pltpu.make_async_copy(coadd, coadd_out, local_sem.at[9 + n_epoch])
    last.start()

    for step in range(n_epoch):
        for ds, db in STEPS:
            if step == 0 and ds == 0 and db == 0:
                continue
            guarded(
                there(ds, db),
                lambda step=step, ds=ds, db=db: piece(step, ds, db, False).wait_send(),
            )
        if step > 0:
            back(0, weight, weight_in, step, False).wait_send()
            back(1, value_out, value_in, step, False).wait_send()
        k = away(step)
        pltpu.make_async_copy(residual.at[k], residual_out.at[k], local_sem.at[9 + k]).wait()
    last.wait()


def leave(residual, coadd, residual_out, coadd_out, images, tiles, sem):
    arrive = [
        pltpu.make_async_copy(residual, images, sem.at[0]),
        pltpu.make_async_copy(coadd, tiles, sem.at[1]),
    ]
    depart = [
        pltpu.make_async_copy(images, residual_out, sem.at[2]),
        pltpu.make_async_copy(tiles, coadd_out, sem.at[3]),
    ]
    for copy in arrive:
        copy.start()
    for i in (1, 0):
        arrive[i].wait()
        depart[i].start()
    for copy in depart:
        copy.wait()


def local(sizes, template, science, variance, bad_mask, intersection, offsets, basis_index, coefficients, basis):
    n_epoch = sizes[0]
    tile_dev, height, width = template.shape
    exp_dev = science.shape[0]
    assert exp_dev == n_epoch
    n_poly = coefficients.shape[2]
    ks = basis.shape[1]
    lanes_all = width + 2 * LANES
    n_pairs = (ks + 1) // 2
    rows_all = -(-n_poly * n_pairs // 8) * 8
    far = pl.BlockSpec(memory_space=pltpu.HBM)
    free = pl.BlockSpec(memory_space=pl.ANY)
    bf16, f32 = jnp.bfloat16, jnp.float32
    dma = pltpu.SemaphoreType.DMA
    offsets = offsets.T
    coefficients = coefficients.transpose(2, 0, 1)
    basis = basis.transpose(1, 2, 0)
    residual, coadd = pl.pallas_call(
        functools.partial(kernel, sizes),
        out_shape=(
            jax.ShapeDtypeStruct(science.shape, f32),
            jax.ShapeDtypeStruct(template.shape, f32),
        ),
        in_specs=[far] * 9,
        out_specs=(free, free),
        scratch_shapes=[
            pltpu.SMEM(intersection.shape, jnp.int32),
            pltpu.SMEM(offsets.shape, jnp.int32),
            pltpu.SMEM(basis_index.shape, jnp.int32),
            pltpu.VMEM(coefficients.shape, f32),
            pltpu.VMEM(template.shape, bf16),
            pltpu.VMEM(science.shape, f32),
            pltpu.VMEM(science.shape, f32),
            pltpu.VMEM(science.shape, jnp.int32),
            pltpu.VMEM(basis.shape, f32),
            pltpu.VMEM(science.shape, f32),
            pltpu.VMEM(template.shape, f32),
            pltpu.VMEM((n_epoch, height, width), bf16),
            pltpu.VMEM((n_epoch, EDGE_ROWS, width), bf16),
            pltpu.VMEM((exp_dev, height, lanes_all), bf16),
            pltpu.VMEM((exp_dev, EDGE_ROWS, lanes_all), bf16),
            pltpu.VMEM((exp_dev, EDGE_ROWS, lanes_all), bf16),
            pltpu.VMEM((n_pairs * LANES, LANES), f32),
            pltpu.VMEM((exp_dev * rows_all, LANES), f32),
            pltpu.VMEM((height * rows_all, LANES), f32),
            pltpu.VMEM((exp_dev, n_poly * height, n_pairs * LANES), bf16),
            pltpu.VMEM((exp_dev, height, width), f32),
            pltpu.VMEM((exp_dev, height, width), f32),
            pltpu.VMEM((exp_dev, height, width), f32),
            pltpu.VMEM((exp_dev, height, width), f32),
            pltpu.VMEM((height, width), f32),
            dma((10 + n_epoch,)),
            dma((n_epoch, 3, 3)),
            dma((n_epoch, 3, 3)),
            dma((2, n_epoch)),
            dma((2, n_epoch)),
        ],
        compiler_params=pltpu.CompilerParams(
            collective_id=0, has_side_effects=True
        ),
    )(
        intersection, offsets, basis_index, coefficients,
        template, science, variance, bad_mask, basis,
    )
    return pl.pallas_call(
        leave,
        out_shape=(
            jax.ShapeDtypeStruct(science.shape, f32),
            jax.ShapeDtypeStruct(template.shape, f32),
        ),
        in_specs=[free] * 2,
        out_specs=(free, free),
        scratch_shapes=[
            pltpu.VMEM(science.shape, f32),
            pltpu.VMEM(template.shape, f32),
            dma((4,)),
        ],
    )(residual, coadd)


def solution(mesh):
    sizes = (mesh.shape["epoch"], mesh.shape["strip"], mesh.shape["band"])
    image = P(("groups", "epoch"), "strip", "band")
    split = ("groups", "epoch")
    in_specs = (
        image, image, image, image, P("groups"),
        P(split, None), P(split, None), P(split, None, None), P(),
    )
    return jax.shard_map(
        functools.partial(local, sizes),
        mesh=mesh,
        in_specs=in_specs,
        out_specs=(image, image),
        check_vma=False,
    )
```

```python
import functools

import jax
import jax.numpy as jnp
from jax import lax
from jax.experimental import pallas as pl
from jax.experimental.pallas import tpu as pltpu
from jax.sharding import PartitionSpec as P

HALF = 9
SHIFT = 4
RIM = HALF + SHIFT
EDGE_ROWS = 16
LANES = 128
SLOT = 64

MESH = pl.DeviceIdType.MESH
STEPS = [(ds, db) for ds in (0, -1, 1) for db in (0, -1, 1)]


def kernel(
    sizes,
    intersection_hbm,
    offsets_hbm,
    basis_index_hbm,
    coefficients_hbm,
    template_hbm,
    science_hbm,
    variance_hbm,
    bad_mask_hbm,
    basis_hbm,
    residual_out,
    coadd_out,
    intersection,
    offsets,
    basis_index,
    coefficients,
    template,
    science,
    variance,
    bad_mask,
    basis,
    residual,
    coadd,
    full,
    bottom,
    mid,
    top,
    low,
    turned_basis,
    pairs,
    turns,
    toeplitz,
    weight,
    weight_in,
    value_out,
    value_in,
    own_value,
    local_sem,
    send_sem,
    recv_sem,
    back_send,
    back_recv,
):
    n_epoch, n_strip, n_band = sizes
    tile_dev, height, width = template.shape
    exp_dev = science.shape[0]
    n_poly, _, n_sel = coefficients.shape
    ks, _, n_basis = basis.shape
    group = lax.axis_index("groups")
    me = lax.axis_index("epoch")
    strip = lax.axis_index("strip")
    band = lax.axis_index("band")

    side = 2 * lax.div(2 * me, n_epoch) - 1

    def away(step):
        return lax.rem(me + n_epoch + side * step, n_epoch)

    def target(epoch, ds, db):
        return (group, epoch, strip + ds, band + db)

    def there(ds, db):
        sides = []
        if ds < 0:
            sides.append(strip >= -ds)
        if ds > 0:
            sides.append(strip < n_strip - ds)
        if db < 0:
            sides.append(band >= -db)
        if db > 0:
            sides.append(band < n_band - db)
        return sides

    def guarded(sides, body):
        if not sides:
            body()
        elif len(sides) == 1:
            pl.when(sides[0])(body)
        else:
            pl.when(jnp.logical_and(sides[0], sides[1]))(body)

    loads = [
        pltpu.make_async_copy(held, here, local_sem.at[i])
        for i, (held, here) in enumerate(
            (
                (basis_hbm, basis),
                (variance_hbm, variance),
                (bad_mask_hbm, bad_mask),
                (science_hbm, science),
                (intersection_hbm, intersection),
                (template_hbm, template),
                (basis_index_hbm, basis_index),
                (coefficients_hbm, coefficients),
                (offsets_hbm, offsets),
            )
        )
    ]
    for i in (4, 5, 6, 7, 0, 1, 2, 3, 8):
        loads[i].start()

    barrier = pltpu.get_barrier_semaphore()
    for ds, db in STEPS:

        def greet(ds=ds, db=db):
            for step in range(n_epoch):
                if step == 0 and ds == 0 and db == 0:
                    continue
                epoch = away(step)
                pl.semaphore_signal(
                    barrier, inc=1, device_id=target(epoch, ds, db), device_id_type=MESH
                )

        guarded(there(ds, db), greet)

    loads[4].wait()
    loads[5].wait()
    for step in range(n_epoch):
        epoch = away(step)
        tile = intersection[epoch * exp_dev + me] - me * tile_dev
        chosen = template[jnp.clip(tile, 0, tile_dev - 1)]
        full[epoch] = chosen
        wide = chosen.astype(jnp.float32)
        bottom[epoch] = wide[height - EDGE_ROWS :].astype(jnp.bfloat16)
    mid[me, :, LANES : LANES + width] = full[me]

    zero = jnp.bfloat16(0)

    @pl.when(strip == 0)
    def _():
        top[...] = jnp.full(top.shape, zero)

    @pl.when(strip == n_strip - 1)
    def _():
        low[...] = jnp.full(low.shape, zero)

    for edge, lanes in ((band == 0, slice(0, LANES)), (band == n_band - 1, slice(LANES + width, None))):

        @pl.when(edge)
        def _(lanes=lanes):
            mid[:, :, lanes] = jnp.full(mid[:, :, lanes].shape, zero)

            @pl.when(strip > 0)
            def _():
                top[:, :, lanes] = jnp.full(top[:, :, lanes].shape, zero)

            @pl.when(strip < n_strip - 1)
            def _():
                low[:, :, lanes] = jnp.full(low[:, :, lanes].shape, zero)

    partners = n_epoch
    if n_strip > 1:
        near = jnp.minimum(strip, 1) + jnp.minimum(n_strip - 1 - strip, 1)
        partners = partners * (1 + near)
    if n_band > 1:
        near = jnp.minimum(band, 1) + jnp.minimum(n_band - 1 - band, 1)
        partners = partners * (1 + near)
    pl.semaphore_wait(barrier, partners - 1)

    def piece(step, ds, db, arriving):
        other = away(step)
        held = {0: slice(0, width), 1: slice(width - LANES, width), -1: slice(0, LANES)}[db]
        lands = {
            0: slice(LANES, LANES + width),
            1: slice(0, LANES),
            -1: slice(LANES + width, 2 * LANES + width),
        }[db]
        slot = other if arriving else me
        source = full.at[other, :, held]
        dest = mid
        if ds == 1:
            source, dest = bottom.at[other, :, held], top
        if ds == -1:
            source, dest = full.at[other, 0:EDGE_ROWS, held], low
        return pltpu.make_async_remote_copy(
            src_ref=source,
            dst_ref=dest.at[slot, :, lands],
            send_sem=send_sem.at[other, ds + 1, db + 1],
            recv_sem=recv_sem.at[slot, ds + 1, db + 1],
            device_id=target(other, ds, db),
            device_id_type=MESH,
        )

    for step in list(range(1, n_epoch)) + [0]:
        for ds, db in STEPS:
            if step == 0 and ds == 0 and db == 0:
                continue
            guarded(there(ds, db), lambda step=step, ds=ds, db=db: piece(step, ds, db, False).start())

    def back(which, out, into, step, arriving):
        other = away(step)
        slot = other if arriving else me
        return pltpu.make_async_remote_copy(
            src_ref=out.at[other],
            dst_ref=into.at[slot],
            send_sem=back_send.at[which, other],
            recv_sem=back_recv.at[which, slot],
            device_id=target(other, 0, 0),
            device_id_type=MESH,
        )

    loads[1].wait()
    loads[2].wait()
    for exposure in range(exp_dev):
        weight[exposure] = bad_mask[exposure].astype(jnp.float32) / variance[exposure]

    loads[6].wait()
    loads[7].wait()
    lane = lax.broadcasted_iota(jnp.int32, (n_poly, LANES), 1)
    mixes = []
    for exposure in range(exp_dev):
        coefs = coefficients[:, exposure, :]
        mix = jnp.zeros((n_poly, LANES), jnp.float32)
        for j in range(n_sel):
            mix = mix + jnp.where(lane == basis_index[exposure, j], coefs[:, j : j + 1], 0.0)
        mixes.append(mix)
        if n_poly < 8:
            mixes.append(jnp.zeros((8 - n_poly, LANES), jnp.float32))
    mixes = jnp.concatenate(mixes, axis=0)

    n_pairs = (ks + 1) // 2
    rows_all = pairs.shape[0] // exp_dev
    turned_basis[...] = jnp.zeros(turned_basis.shape, jnp.float32)
    loads[0].wait()
    for b in range(ks):
        turned_basis[b * SLOT : b * SLOT + ks, 0:n_basis] = basis[:, b, :]

    for q in range(0, n_pairs, 2):
        some = lax.dot_general(
            mixes,
            turned_basis[q * LANES : (q + 2) * LANES, :],
            (((1,), (1,)), ((), ())),
            precision=lax.Precision.HIGHEST,
            preferred_element_type=jnp.float32,
        )
        some = some.astype(jnp.bfloat16).astype(jnp.float32)
        for half in range(2):
            for exposure in range(exp_dev):
                at = exposure * rows_all + (q + half) * n_poly
                pairs[at : at + n_poly, :] = some[
                    exposure * 8 : exposure * 8 + n_poly, half * LANES : (half + 1) * LANES
                ]

    for step in range(1, n_epoch):
        back(0, weight, weight_in, step, False).start()

    loads[8].wait()

    def build(exposure, carry):
        shift = offsets[0, exposure] + (SHIFT + EDGE_ROWS - RIM)
        every = pairs[pl.ds(pl.multiple_of(exposure * rows_all, 8), rows_all), :]
        for y in range(height):
            turns[y * rows_all : (y + 1) * rows_all, :] = pltpu.roll(every, shift + y, 1)
        for p in range(0, n_poly, 2):
            for q in range(n_pairs):
                halves = [
                    turns[pl.ds(q * n_poly + p + h, height, stride=rows_all), :]
                    for h in range(2)
                ]
                toeplitz[
                    exposure, p * height : (p + 2) * height, q * LANES : (q + 1) * LANES
                ] = jnp.concatenate(halves, axis=0).astype(jnp.bfloat16)
        return carry

    lax.fori_loop(0, exp_dev, build, 0)

    row = lax.broadcasted_iota(jnp.int32, (height, 1), 0) + strip * height
    col = lax.broadcasted_iota(jnp.int32, (1, width), 1) + band * width
    r = (2.0 * row.astype(jnp.float32) + 1.0) / (height * n_strip) - 1.0
    c = (2.0 * col.astype(jnp.float32) + 1.0) / (width * n_band) - 1.0
    r = jnp.broadcast_to(r, (height, width))
    c = jnp.broadcast_to(c, (height, width))

    def arrive(step):
        for ds, db in STEPS:
            if ds == 0 and db == 0 and step == 0:
                continue
            guarded(
                there(-ds, -db),
                lambda ds=ds, db=db: piece(step, ds, db, True).wait_recv(),
            )

    loads[3].wait()
    for step in range(n_epoch):
        k = away(step)
        arrive(step)
        slab = jnp.concatenate(
            [
                top[k].astype(jnp.float32),
                mid[k].astype(jnp.float32),
                low[k].astype(jnp.float32),
                jnp.zeros((SLOT - height - 2 * EDGE_ROWS, width + 2 * LANES), jnp.float32),
            ],
            axis=0,
        )
        total = width + 2 * LANES
        slab = pltpu.roll(slab, total - (LANES - RIM + SHIFT) - offsets[1, k], 1)
        slab = slab[:, : width + LANES].astype(jnp.bfloat16)
        conv = jnp.zeros((n_poly * height, width), jnp.float32)
        for first in range(0, ks, 4):
            columns = range(first, min(first + 4, ks))
            stacked = jnp.concatenate([slab[:, b : b + width] for b in columns], axis=0)
            conv = conv + jnp.dot(
                toeplitz[k, :, first * SLOT : (first + len(columns)) * SLOT],
                stacked,
                preferred_element_type=jnp.float32,
            )
        q = [conv[p * height : (p + 1) * height] for p in range(n_poly)]
        model = q[0] + r * (q[1] + r * q[3] + c * q[4]) + c * (q[2] + c * q[5])
        left = science[k] - model
        residual[k] = left
        pltpu.make_async_copy(residual.at[k], residual_out.at[k], local_sem.at[9 + k]).start()
        value = weight[k] * left
        if step == 0:
            own_value[...] = value
        else:
            value_out[k] = value
            back(1, value_out, value_in, step, False).start()

    numer = [None] * tile_dev
    denom = [None] * tile_dev
    for step in range(n_epoch):
        k = away(step)
        tile = intersection[k * exp_dev + me] - me * tile_dev
        if step == 0:
            upper, under = own_value[...], weight[me]
        else:
            back(0, weight, weight_in, step, True).wait_recv()
            back(1, value_out, value_in, step, True).wait_recv()
            upper = value_in[k]
            under = weight_in[k]
        for t in range(tile_dev):
            here = (tile == t).astype(jnp.float32)
            numer[t] = upper * here if step == 0 else numer[t] + upper * here
            denom[t] = under * here if step == 0 else denom[t] + under * here
    for t in range(tile_dev):
        coadd[t] = numer[t] / (denom[t] + 1.0)
    last = pltpu.make_async_copy(coadd, coadd_out, local_sem.at[9 + n_epoch])
    last.start()

    for step in range(n_epoch):
        for ds, db in STEPS:
            if step == 0 and ds == 0 and db == 0:
                continue
            guarded(
                there(ds, db),
                lambda step=step, ds=ds, db=db: piece(step, ds, db, False).wait_send(),
            )
        if step > 0:
            back(0, weight, weight_in, step, False).wait_send()
            back(1, value_out, value_in, step, False).wait_send()
        k = away(step)
        pltpu.make_async_copy(residual.at[k], residual_out.at[k], local_sem.at[9 + k]).wait()
    last.wait()


def leave(residual, coadd, residual_out, coadd_out, images, tiles, sem):
    parts = [
        (held.at[i], here.at[i], out.at[i])
        for held, here, out in ((residual, images, residual_out), (coadd, tiles, coadd_out))
        for i in range(here.shape[0])
    ]
    arrive = [
        pltpu.make_async_copy(held, here, sem.at[0, i]) for i, (held, here, _) in enumerate(parts)
    ]
    depart = [
        pltpu.make_async_copy(here, out, sem.at[1, i]) for i, (_, here, out) in enumerate(parts)
    ]
    for copy in arrive:
        copy.start()
    for i in range(len(parts)):
        arrive[i].wait()
        depart[i].start()
    for copy in depart:
        copy.wait()


def local(sizes, template, science, variance, bad_mask, intersection, offsets, basis_index, coefficients, basis):
    n_epoch = sizes[0]
    tile_dev, height, width = template.shape
    exp_dev = science.shape[0]
    assert exp_dev == n_epoch
    n_poly = coefficients.shape[2]
    ks = basis.shape[1]
    lanes_all = width + 2 * LANES
    n_pairs = (ks + 1) // 2
    rows_all = -(-n_poly * n_pairs // 8) * 8
    far = pl.BlockSpec(memory_space=pltpu.HBM)
    free = pl.BlockSpec(memory_space=pl.ANY)
    bf16, f32 = jnp.bfloat16, jnp.float32
    dma = pltpu.SemaphoreType.DMA
    offsets = offsets.T
    coefficients = coefficients.transpose(2, 0, 1)
    basis = basis.transpose(1, 2, 0)
    residual, coadd = pl.pallas_call(
        functools.partial(kernel, sizes),
        out_shape=(
            jax.ShapeDtypeStruct(science.shape, f32),
            jax.ShapeDtypeStruct(template.shape, f32),
        ),
        in_specs=[far] * 9,
        out_specs=(free, free),
        scratch_shapes=[
            pltpu.SMEM(intersection.shape, jnp.int32),
            pltpu.SMEM(offsets.shape, jnp.int32),
            pltpu.SMEM(basis_index.shape, jnp.int32),
            pltpu.VMEM(coefficients.shape, f32),
            pltpu.VMEM(template.shape, bf16),
            pltpu.VMEM(science.shape, f32),
            pltpu.VMEM(science.shape, f32),
            pltpu.VMEM(science.shape, jnp.int32),
            pltpu.VMEM(basis.shape, f32),
            pltpu.VMEM(science.shape, f32),
            pltpu.VMEM(template.shape, f32),
            pltpu.VMEM((n_epoch, height, width), bf16),
            pltpu.VMEM((n_epoch, EDGE_ROWS, width), bf16),
            pltpu.VMEM((exp_dev, height, lanes_all), bf16),
            pltpu.VMEM((exp_dev, EDGE_ROWS, lanes_all), bf16),
            pltpu.VMEM((exp_dev, EDGE_ROWS, lanes_all), bf16),
            pltpu.VMEM((n_pairs * LANES, LANES), f32),
            pltpu.VMEM((exp_dev * rows_all, LANES), f32),
            pltpu.VMEM((height * rows_all, LANES), f32),
            pltpu.VMEM((exp_dev, n_poly * height, n_pairs * LANES), bf16),
            pltpu.VMEM((exp_dev, height, width), f32),
            pltpu.VMEM((exp_dev, height, width), f32),
            pltpu.VMEM((exp_dev, height, width), f32),
            pltpu.VMEM((exp_dev, height, width), f32),
            pltpu.VMEM((height, width), f32),
            dma((10 + n_epoch,)),
            dma((n_epoch, 3, 3)),
            dma((n_epoch, 3, 3)),
            dma((2, n_epoch)),
            dma((2, n_epoch)),
        ],
        compiler_params=pltpu.CompilerParams(
            collective_id=0, has_side_effects=True
        ),
    )(
        intersection, offsets, basis_index, coefficients,
        template, science, variance, bad_mask, basis,
    )
    return pl.pallas_call(
        leave,
        out_shape=(
            jax.ShapeDtypeStruct(science.shape, f32),
            jax.ShapeDtypeStruct(template.shape, f32),
        ),
        in_specs=[free] * 2,
        out_specs=(free, free),
        scratch_shapes=[
            pltpu.VMEM(science.shape, f32),
            pltpu.VMEM(template.shape, f32),
            dma((2, exp_dev + tile_dev)),
        ],
    )(residual, coadd)


def solution(mesh):
    sizes = (mesh.shape["epoch"], mesh.shape["strip"], mesh.shape["band"])
    image = P(("groups", "epoch"), "strip", "band")
    split = ("groups", "epoch")
    in_specs = (
        image, image, image, image, P("groups"),
        P(split, None), P(split, None), P(split, None, None), P(),
    )
    return jax.shard_map(
        functools.partial(local, sizes),
        mesh=mesh,
        in_specs=in_specs,
        out_specs=(image, image),
        check_vma=False,
    )
```

```python
import functools

import jax
import jax.numpy as jnp
from jax import lax
from jax.experimental import pallas as pl
from jax.experimental.pallas import tpu as pltpu
from jax.sharding import PartitionSpec as P

HALF = 9
SHIFT = 4
RIM = HALF + SHIFT
EDGE_ROWS = 16
LANES = 128
SLOT = 64

MESH = pl.DeviceIdType.MESH
STEPS = [(ds, db) for ds in (-1, 1, 0) for db in (-1, 1, 0)]


def kernel(
    sizes,
    intersection_hbm,
    offsets_hbm,
    basis_index_hbm,
    coefficients_hbm,
    template_hbm,
    science_hbm,
    variance_hbm,
    bad_mask_hbm,
    basis_hbm,
    residual_out,
    coadd_out,
    intersection,
    offsets,
    basis_index,
    coefficients,
    template,
    science,
    variance,
    bad_mask,
    basis,
    residual,
    coadd,
    full,
    bottom,
    mid,
    top,
    low,
    turned_basis,
    pairs,
    turns,
    toeplitz,
    weight,
    weight_in,
    value_out,
    value_in,
    own_value,
    local_sem,
    send_sem,
    recv_sem,
    back_send,
    back_recv,
):
    n_epoch, n_strip, n_band = sizes
    tile_dev, height, width = template.shape
    exp_dev = science.shape[0]
    n_poly, _, n_sel = coefficients.shape
    ks, _, n_basis = basis.shape
    group = lax.axis_index("groups")
    me = lax.axis_index("epoch")
    strip = lax.axis_index("strip")
    band = lax.axis_index("band")

    side = 2 * lax.div(2 * me, n_epoch) - 1

    def away(step):
        return lax.rem(me + n_epoch + side * step, n_epoch)

    def target(epoch, ds, db):
        return (group, epoch, strip + ds, band + db)

    def there(ds, db):
        sides = []
        if ds < 0:
            sides.append(strip >= -ds)
        if ds > 0:
            sides.append(strip < n_strip - ds)
        if db < 0:
            sides.append(band >= -db)
        if db > 0:
            sides.append(band < n_band - db)
        return sides

    def guarded(sides, body):
        if not sides:
            body()
        elif len(sides) == 1:
            pl.when(sides[0])(body)
        else:
            pl.when(jnp.logical_and(sides[0], sides[1]))(body)

    loads = [
        pltpu.make_async_copy(held, here, local_sem.at[i])
        for i, (held, here) in enumerate(
            (
                (basis_hbm, basis),
                (variance_hbm, variance),
                (bad_mask_hbm, bad_mask),
                (science_hbm, science),
                (intersection_hbm, intersection),
                (template_hbm, template),
                (basis_index_hbm, basis_index),
                (coefficients_hbm, coefficients),
                (offsets_hbm, offsets),
            )
        )
    ]
    for i in (4, 5, 6, 7, 0, 1, 2, 3, 8):
        loads[i].start()

    barrier = pltpu.get_barrier_semaphore()
    for ds, db in STEPS:

        def greet(ds=ds, db=db):
            for step in range(n_epoch):
                if step == 0 and ds == 0 and db == 0:
                    continue
                epoch = away(step)
                pl.semaphore_signal(
                    barrier, inc=1, device_id=target(epoch, ds, db), device_id_type=MESH
                )

        guarded(there(ds, db), greet)

    loads[4].wait()
    loads[5].wait()
    for step in range(n_epoch):
        epoch = away(step)
        tile = intersection[epoch * exp_dev + me] - me * tile_dev
        chosen = template[jnp.clip(tile, 0, tile_dev - 1)]
        full[epoch] = chosen
        wide = chosen.astype(jnp.float32)
        bottom[epoch] = wide[height - EDGE_ROWS :].astype(jnp.bfloat16)
    mid[me, :, LANES : LANES + width] = full[me]

    zero = jnp.bfloat16(0)

    @pl.when(strip == 0)
    def _():
        top[...] = jnp.full(top.shape, zero)

    @pl.when(strip == n_strip - 1)
    def _():
        low[...] = jnp.full(low.shape, zero)

    for edge, lanes in ((band == 0, slice(0, LANES)), (band == n_band - 1, slice(LANES + width, None))):

        @pl.when(edge)
        def _(lanes=lanes):
            mid[:, :, lanes] = jnp.full(mid[:, :, lanes].shape, zero)

            @pl.when(strip > 0)
            def _():
                top[:, :, lanes] = jnp.full(top[:, :, lanes].shape, zero)

            @pl.when(strip < n_strip - 1)
            def _():
                low[:, :, lanes] = jnp.full(low[:, :, lanes].shape, zero)

    partners = n_epoch
    if n_strip > 1:
        near = jnp.minimum(strip, 1) + jnp.minimum(n_strip - 1 - strip, 1)
        partners = partners * (1 + near)
    if n_band > 1:
        near = jnp.minimum(band, 1) + jnp.minimum(n_band - 1 - band, 1)
        partners = partners * (1 + near)
    pl.semaphore_wait(barrier, partners - 1)

    def piece(step, ds, db, arriving):
        other = away(step)
        held = {0: slice(0, width), 1: slice(width - LANES, width), -1: slice(0, LANES)}[db]
        lands = {
            0: slice(LANES, LANES + width),
            1: slice(0, LANES),
            -1: slice(LANES + width, 2 * LANES + width),
        }[db]
        slot = other if arriving else me
        source = full.at[other, :, held]
        dest = mid
        if ds == 1:
            source, dest = bottom.at[other, :, held], top
        if ds == -1:
            source, dest = full.at[other, 0:EDGE_ROWS, held], low
        return pltpu.make_async_remote_copy(
            src_ref=source,
            dst_ref=dest.at[slot, :, lands],
            send_sem=send_sem.at[other, ds + 1, db + 1],
            recv_sem=recv_sem.at[slot, ds + 1, db + 1],
            device_id=target(other, ds, db),
            device_id_type=MESH,
        )

    for step in list(range(1, n_epoch)) + [0]:
        for ds, db in STEPS:
            if step == 0 and ds == 0 and db == 0:
                continue
            guarded(there(ds, db), lambda step=step, ds=ds, db=db: piece(step, ds, db, False).start())

    def back(which, out, into, step, arriving):
        other = away(step)
        slot = other if arriving else me
        return pltpu.make_async_remote_copy(
            src_ref=out.at[other],
            dst_ref=into.at[slot],
            send_sem=back_send.at[which, other],
            recv_sem=back_recv.at[which, slot],
            device_id=target(other, 0, 0),
            device_id_type=MESH,
        )

    loads[1].wait()
    loads[2].wait()
    for exposure in range(exp_dev):
        weight[exposure] = bad_mask[exposure].astype(jnp.float32) / variance[exposure]

    loads[6].wait()
    loads[7].wait()
    lane = lax.broadcasted_iota(jnp.int32, (n_poly, LANES), 1)
    mixes = []
    for exposure in range(exp_dev):
        coefs = coefficients[:, exposure, :]
        mix = jnp.zeros((n_poly, LANES), jnp.float32)
        for j in range(n_sel):
            mix = mix + jnp.where(lane == basis_index[exposure, j], coefs[:, j : j + 1], 0.0)
        mixes.append(mix)
        if n_poly < 8:
            mixes.append(jnp.zeros((8 - n_poly, LANES), jnp.float32))
    mixes = jnp.concatenate(mixes, axis=0)

    n_pairs = (ks + 1) // 2
    rows_all = pairs.shape[0] // exp_dev
    turned_basis[...] = jnp.zeros(turned_basis.shape, jnp.float32)
    loads[0].wait()
    for b in range(ks):
        turned_basis[b * SLOT : b * SLOT + ks, 0:n_basis] = basis[:, b, :]

    for q in range(0, n_pairs, 2):
        some = lax.dot_general(
            mixes,
            turned_basis[q * LANES : (q + 2) * LANES, :],
            (((1,), (1,)), ((), ())),
            precision=lax.Precision.HIGHEST,
            preferred_element_type=jnp.float32,
        )
        some = some.astype(jnp.bfloat16).astype(jnp.float32)
        for half in range(2):
            for exposure in range(exp_dev):
                at = exposure * rows_all + (q + half) * n_poly
                pairs[at : at + n_poly, :] = some[
                    exposure * 8 : exposure * 8 + n_poly, half * LANES : (half + 1) * LANES
                ]

    for step in range(1, n_epoch):
        back(0, weight, weight_in, step, False).start()

    loads[8].wait()

    def build(exposure, carry):
        shift = offsets[0, exposure] + (SHIFT + EDGE_ROWS - RIM)
        every = pairs[pl.ds(pl.multiple_of(exposure * rows_all, 8), rows_all), :]
        for y in range(height):
            turns[y * rows_all : (y + 1) * rows_all, :] = pltpu.roll(every, shift + y, 1)
        for p in range(0, n_poly, 2):
            for q in range(n_pairs):
                halves = [
                    turns[pl.ds(q * n_poly + p + h, height, stride=rows_all), :]
                    for h in range(2)
                ]
                toeplitz[
                    exposure, p * height : (p + 2) * height, q * LANES : (q + 1) * LANES
                ] = jnp.concatenate(halves, axis=0).astype(jnp.bfloat16)
        return carry

    lax.fori_loop(0, exp_dev, build, 0)

    row = lax.broadcasted_iota(jnp.int32, (height, 1), 0) + strip * height
    col = lax.broadcasted_iota(jnp.int32, (1, width), 1) + band * width
    r = (2.0 * row.astype(jnp.float32) + 1.0) / (height * n_strip) - 1.0
    c = (2.0 * col.astype(jnp.float32) + 1.0) / (width * n_band) - 1.0
    r = jnp.broadcast_to(r, (height, width))
    c = jnp.broadcast_to(c, (height, width))

    def arrive(step):
        for ds, db in STEPS:
            if ds == 0 and db == 0 and step == 0:
                continue
            guarded(
                there(-ds, -db),
                lambda ds=ds, db=db: piece(step, ds, db, True).wait_recv(),
            )

    loads[3].wait()
    for step in range(n_epoch):
        k = away(step)
        arrive(step)
        slab = jnp.concatenate(
            [
                top[k].astype(jnp.float32),
                mid[k].astype(jnp.float32),
                low[k].astype(jnp.float32),
                jnp.zeros((SLOT - height - 2 * EDGE_ROWS, width + 2 * LANES), jnp.float32),
            ],
            axis=0,
        )
        total = width + 2 * LANES
        slab = pltpu.roll(slab, total - (LANES - RIM + SHIFT) - offsets[1, k], 1)
        slab = slab[:, : width + LANES].astype(jnp.bfloat16)
        conv = jnp.zeros((n_poly * height, width), jnp.float32)
        for first in range(0, ks, 4):
            columns = range(first, min(first + 4, ks))
            stacked = jnp.concatenate([slab[:, b : b + width] for b in columns], axis=0)
            conv = conv + jnp.dot(
                toeplitz[k, :, first * SLOT : (first + len(columns)) * SLOT],
                stacked,
                preferred_element_type=jnp.float32,
            )
        q = [conv[p * height : (p + 1) * height] for p in range(n_poly)]
        model = q[0] + r * (q[1] + r * q[3] + c * q[4]) + c * (q[2] + c * q[5])
        left = science[k] - model
        residual[k] = left
        pltpu.make_async_copy(residual.at[k], residual_out.at[k], local_sem.at[9 + k]).start()
        value = weight[k] * left
        if step == 0:
            own_value[...] = value
        else:
            value_out[k] = value
            back(1, value_out, value_in, step, False).start()

    numer = [None] * tile_dev
    denom = [None] * tile_dev
    for step in range(n_epoch):
        k = away(step)
        tile = intersection[k * exp_dev + me] - me * tile_dev
        if step == 0:
            upper, under = own_value[...], weight[me]
        else:
            back(0, weight, weight_in, step, True).wait_recv()
            back(1, value_out, value_in, step, True).wait_recv()
            upper = value_in[k]
            under = weight_in[k]
        for t in range(tile_dev):
            here = (tile == t).astype(jnp.float32)
            numer[t] = upper * here if step == 0 else numer[t] + upper * here
            denom[t] = under * here if step == 0 else denom[t] + under * here
    for t in range(tile_dev):
        coadd[t] = numer[t] / (denom[t] + 1.0)
    last = pltpu.make_async_copy(coadd, coadd_out, local_sem.at[9 + n_epoch])
    last.start()

    for step in range(n_epoch):
        for ds, db in STEPS:
            if step == 0 and ds == 0 and db == 0:
                continue
            guarded(
                there(ds, db),
                lambda step=step, ds=ds, db=db: piece(step, ds, db, False).wait_send(),
            )
        if step > 0:
            back(0, weight, weight_in, step, False).wait_send()
            back(1, value_out, value_in, step, False).wait_send()
        k = away(step)
        pltpu.make_async_copy(residual.at[k], residual_out.at[k], local_sem.at[9 + k]).wait()
    last.wait()


def leave(residual, coadd, residual_out, coadd_out, images, tiles, sem):
    parts = [
        (held.at[i], here.at[i], out.at[i])
        for held, here, out in ((residual, images, residual_out), (coadd, tiles, coadd_out))
        for i in range(here.shape[0])
    ]
    arrive = [
        pltpu.make_async_copy(held, here, sem.at[0, i]) for i, (held, here, _) in enumerate(parts)
    ]
    depart = [
        pltpu.make_async_copy(here, out, sem.at[1, i]) for i, (_, here, out) in enumerate(parts)
    ]
    for copy in arrive:
        copy.start()
    for i in range(len(parts)):
        arrive[i].wait()
        depart[i].start()
    for copy in depart:
        copy.wait()


def local(sizes, template, science, variance, bad_mask, intersection, offsets, basis_index, coefficients, basis):
    n_epoch = sizes[0]
    tile_dev, height, width = template.shape
    exp_dev = science.shape[0]
    assert exp_dev == n_epoch
    n_poly = coefficients.shape[2]
    ks = basis.shape[1]
    lanes_all = width + 2 * LANES
    n_pairs = (ks + 1) // 2
    rows_all = -(-n_poly * n_pairs // 8) * 8
    far = pl.BlockSpec(memory_space=pltpu.HBM)
    free = pl.BlockSpec(memory_space=pl.ANY)
    bf16, f32 = jnp.bfloat16, jnp.float32
    dma = pltpu.SemaphoreType.DMA
    offsets = offsets.T
    coefficients = coefficients.transpose(2, 0, 1)
    basis = basis.transpose(1, 2, 0)
    residual, coadd = pl.pallas_call(
        functools.partial(kernel, sizes),
        out_shape=(
            jax.ShapeDtypeStruct(science.shape, f32),
            jax.ShapeDtypeStruct(template.shape, f32),
        ),
        in_specs=[far] * 9,
        out_specs=(free, free),
        scratch_shapes=[
            pltpu.SMEM(intersection.shape, jnp.int32),
            pltpu.SMEM(offsets.shape, jnp.int32),
            pltpu.SMEM(basis_index.shape, jnp.int32),
            pltpu.VMEM(coefficients.shape, f32),
            pltpu.VMEM(template.shape, bf16),
            pltpu.VMEM(science.shape, f32),
            pltpu.VMEM(science.shape, f32),
            pltpu.VMEM(science.shape, jnp.int32),
            pltpu.VMEM(basis.shape, f32),
            pltpu.VMEM(science.shape, f32),
            pltpu.VMEM(template.shape, f32),
            pltpu.VMEM((n_epoch, height, width), bf16),
            pltpu.VMEM((n_epoch, EDGE_ROWS, width), bf16),
            pltpu.VMEM((exp_dev, height, lanes_all), bf16),
            pltpu.VMEM((exp_dev, EDGE_ROWS, lanes_all), bf16),
            pltpu.VMEM((exp_dev, EDGE_ROWS, lanes_all), bf16),
            pltpu.VMEM((n_pairs * LANES, LANES), f32),
            pltpu.VMEM((exp_dev * rows_all, LANES), f32),
            pltpu.VMEM((height * rows_all, LANES), f32),
            pltpu.VMEM((exp_dev, n_poly * height, n_pairs * LANES), bf16),
            pltpu.VMEM((exp_dev, height, width), f32),
            pltpu.VMEM((exp_dev, height, width), f32),
            pltpu.VMEM((exp_dev, height, width), f32),
            pltpu.VMEM((exp_dev, height, width), f32),
            pltpu.VMEM((height, width), f32),
            dma((10 + n_epoch,)),
            dma((n_epoch, 3, 3)),
            dma((n_epoch, 3, 3)),
            dma((2, n_epoch)),
            dma((2, n_epoch)),
        ],
        compiler_params=pltpu.CompilerParams(
            collective_id=0, has_side_effects=True
        ),
    )(
        intersection, offsets, basis_index, coefficients,
        template, science, variance, bad_mask, basis,
    )
    return pl.pallas_call(
        leave,
        out_shape=(
            jax.ShapeDtypeStruct(science.shape, f32),
            jax.ShapeDtypeStruct(template.shape, f32),
        ),
        in_specs=[free] * 2,
        out_specs=(free, free),
        scratch_shapes=[
            pltpu.VMEM(science.shape, f32),
            pltpu.VMEM(template.shape, f32),
            dma((2, exp_dev + tile_dev)),
        ],
    )(residual, coadd)


def solution(mesh):
    sizes = (mesh.shape["epoch"], mesh.shape["strip"], mesh.shape["band"])
    image = P(("groups", "epoch"), "strip", "band")
    split = ("groups", "epoch")
    in_specs = (
        image, image, image, image, P("groups"),
        P(split, None), P(split, None), P(split, None, None), P(),
    )
    return jax.shard_map(
        functools.partial(local, sizes),
        mesh=mesh,
        in_specs=in_specs,
        out_specs=(image, image),
        check_vma=False,
    )
```
